32 devices in a mesh: scen: 4 (over y, core), node: 8 (over z, x).
Axes of the slice: x: 2, y: 2, z: 4, core: 2. Of those that a mesh axis runs over, the one named last changes fastest.
Arguments:
- factors: bfloat16 [8, 4, 1024, 1024], P('node', 'scen'), may hold values from -0.1875 to 0.1875
- couple: bfloat16 [8, 4, 1024, 512], P('node', 'scen'), may hold values from -0.1875 to 0.1875
- leaf_rhs: bfloat16 [8, 4, 2, 1024], P('node', 'scen'), may hold values from -6 to 6
- node_diag: float32 [8, 512, 512], P('node', 'scen'), as said below
- node_rhs: float32 [8, 2, 512], P('node', None, 'scen'), may hold values from -6 to 6
- link_root: float32 [8, 512, 512], P('node', 'scen'), may hold values from -1.5 to 1.5
- root_diag: float32 [512, 512], replicated, as said below
- root_rhs: float32 [2, 512], replicated, may hold values from -6 to 6
Outputs:
- leaf_solution: float32 [8, 4, 2, 1024], P('node', 'scen')
- node_solution: float32 [8, 2, 512], P('node', None, 'scen')
- root_solution: float32 [2, 512], replicated
The draws below stay inside these ranges and needn't reach their ends.
Inputs may be any that keep to these rules, and one draw needn't show every extreme that they name: `node_diag`: symmetric positive definite. `root_diag`: symmetric positive definite.
All inputs are finite; a program needn't handle non-finite values.
Results may differ from the reference program's by a relative error of at most 0.0036.
Values sent between devices are 32-bit elements; how exact they have to be, the bound alone decides.
No kernel may reach another device: no remote copies, remote signals or barrier semaphores. Data moves between devices by JAX's collectives and lax.ppermute only.
A program may use at most 64 MiB of HBM per device.

```python
import jax
import jax.numpy as jnp
from jax import lax

KO = 1024
LINK = 512
NODES = 8
SUB = 4


def definite(key, count, order, lower_eig, upper_eig):
    first, second = jax.random.split(jax.random.fold_in(key, 11))
    columns = 2 * order
    basis = jax.random.normal(first, (count, order, columns), jnp.float32)
    levels = jnp.exp(jax.random.uniform(second, (count, columns), jnp.float32, jnp.log(lower_eig), jnp.log(upper_eig)))
    weighted = basis * levels[:, None, :]
    product = jnp.einsum('nik,njk->nij', weighted, basis, precision=lax.Precision.HIGHEST) / columns
    return 0.5 * (product + jnp.swapaxes(product, 1, 2))


def draw_node_diag(key, part):
    return definite(key, NODES, LINK, 1.0, 4000.0)


def draw_root_diag(key, part):
    return definite(key, 1, LINK, 2.0, 8000.0)[0]


def shard_levels(rng, dims, shards, smallest, largest):
    gain, own = 1.0, jax.random.fold_in(rng, 6)
    for position, shards_of in shards:
        steps = jnp.exp(jax.random.uniform(jax.random.fold_in(own, position), (shards_of,), jnp.float32, smallest / len(shards), largest / len(shards)))
        gain = gain * jnp.repeat(steps, dims[position] // shards_of).reshape([-1 if axis == position else 1 for axis in range(len(dims))])
    return gain


def centred(rng, shape, deviation, most, pieces=(), kind=jnp.bfloat16):
    array = jax.random.normal(rng, shape, jnp.float32) * deviation
    if len(pieces) > 0:
        array = shard_levels(rng, shape, pieces, -0.22, 0.18) * array
    return jnp.clip(array, min=-most, max=most).astype(kind)


def setup_inputs(seed: int = 0) -> dict:
    key_of = jax.random.split(jax.random.key(seed), 9)
    factors = centred(key_of[0], (NODES, SUB, KO, KO), KO ** -0.5, 0.1875, ((0, 8), (1, 4)))
    couple = centred(key_of[1], (NODES, SUB, KO, LINK), KO ** -0.5, 0.1875, ((0, 8), (1, 4)))
    leaf_rhs = centred(key_of[2], (NODES, SUB, 2, KO), 1.0, 6.0, ((0, 8), (1, 4)))
    node_diag = draw_node_diag(jax.random.fold_in(key_of[8], 71), 0)
    node_rhs = centred(key_of[4], (NODES, 2, LINK), 1.0, 6.0, ((0, 8), (2, 4)), jnp.float32)
    link_root = centred(key_of[5], (NODES, LINK, LINK), 16 ** -0.5, 1.5, ((0, 8), (1, 4)), jnp.float32)
    root_diag = draw_root_diag(jax.random.fold_in(key_of[8], 71), 0)
    root_rhs = centred(key_of[7], (2, LINK), 1.0, 6.0, (), jnp.float32)
    return dict(factors=factors, couple=couple, leaf_rhs=leaf_rhs, node_diag=node_diag, node_rhs=node_rhs, link_root=link_root, root_diag=root_diag, root_rhs=root_rhs)


HIGH = lax.Precision.HIGHEST

def leaf_terms(factor, coupling, rights):
    wide_factor = factor.astype(jnp.float32)
    reduced = jnp.dot(wide_factor.T, coupling.astype(jnp.float32), precision=HIGH).astype(jnp.bfloat16)
    projected = jnp.dot(rights.astype(jnp.float32), wide_factor, precision=HIGH)
    wide_reduced = reduced.astype(jnp.float32)
    schur = jnp.dot(wide_reduced.T, wide_reduced, precision=HIGH)
    rounded = lax.optimization_barrier(projected.astype(jnp.bfloat16)).astype(jnp.float32)
    vector = jnp.dot(rounded, wide_reduced, precision=HIGH)
    return (reduced, projected, schur, vector)

def node_section(packed):
    factor_set, coupling_set, rights_set, diag_block, node_vec, root_link = packed
    reduced, projected, schur, vector = jax.vmap(leaf_terms)(factor_set, coupling_set, rights_set)
    node_matrix = diag_block + jnp.sum(schur, axis=0)
    node_vector = node_vec + jnp.sum(vector, axis=0)
    lower = jnp.linalg.cholesky(node_matrix)
    solved_link = jax.scipy.linalg.cho_solve((lower, True), root_link)
    solved_rhs = jax.scipy.linalg.cho_solve((lower, True), node_vector.T)
    root_part = jnp.dot(root_link.T, solved_link, precision=HIGH)
    root_vec = jnp.dot(root_link.T, solved_rhs, precision=HIGH)
    return (lower, node_vector, root_part, root_vec)

def back_section(packed):
    factor_set, coupling_set, rights_set, lower, node_vector, root_link, root_sol = packed
    shifted = node_vector.T - jnp.dot(root_link, root_sol, precision=HIGH)
    node_sol = jax.scipy.linalg.cho_solve((lower, True), shifted)
    node_low = node_sol.astype(jnp.bfloat16).astype(jnp.float32)

    def one_leaf(factor, coupling, rights):
        reduced, projected, schur, vector = leaf_terms(factor, coupling, rights)
        update = jnp.dot(reduced.astype(jnp.float32), node_low, precision=HIGH)
        difference = (update.T - projected).astype(jnp.bfloat16).astype(jnp.float32)
        return jnp.dot(difference, factor.astype(jnp.float32).T, precision=HIGH)
    leaves = jax.vmap(one_leaf)(factor_set, coupling_set, rights_set)
    return (leaves, node_sol.T)

def reference(factors, couple, leaf_rhs, node_diag, node_rhs, link_root, root_diag, root_rhs):
    lowers, vectors, root_parts, root_vecs = lax.map(node_section, (factors, couple, leaf_rhs, node_diag, node_rhs, link_root))
    root_matrix = root_diag + jnp.sum(root_parts, axis=0)
    root_vector = jnp.sum(root_vecs, axis=0) - root_rhs.T
    root_lower = jnp.linalg.cholesky(root_matrix)
    root_sol = jax.scipy.linalg.cho_solve((root_lower, True), root_vector)

    def back_node(packed):
        return back_section(packed + (root_sol,))
    leaves, nodes = lax.map(back_node, (factors, couple, leaf_rhs, lowers, vectors, link_root))
    return (leaves, nodes, root_sol.T)
```

```python
import jax
import jax.numpy as jnp
from jax import lax
from jax.experimental import pallas as pl
from jax.experimental.pallas import tpu as pltpu
from jax.sharding import PartitionSpec as P

F32, BF16 = jnp.float32, jnp.bfloat16
NN, NT, TN = ((1,), (0,)), ((1,), (1,)), ((0,), (0,))
ROWS = 8
PARTS = 4
NEAR = 2


def dot(a, b, dims):
    return lax.dot_general(a, b, (dims, ((), ())), preferred_element_type=F32)


def thirds(x):
    high = x.astype(BF16)
    rest = x - high.astype(F32)
    mid = rest.astype(BF16)
    return high, mid, (rest - mid.astype(F32)).astype(BF16)


def exact(a, b, dims):
    (ah, am, al), (bh, bm, bl) = thirds(a), thirds(b)
    left = jnp.concatenate([ah, ah, am, am, ah, al], dims[0][0])
    right = jnp.concatenate([bh, bm, bh, bm, bl, bh], dims[1][0])
    return dot(left, right, dims)


def rank_update(u):
    high = u.astype(BF16).astype(F32)
    rest = u - high
    mid = rest.astype(BF16).astype(F32)
    low = rest - mid
    left = jnp.concatenate([high, high, mid, mid, high, low], 0).astype(BF16)
    right = jnp.concatenate([high, mid, high, mid, low, high], 0).astype(BF16)
    return dot(left, right, TN)


def from_lane(x, i):
    return jnp.broadcast_to(x[:, i : i + 1], x.shape)


def from_row(x, i):
    return jnp.take_along_axis(x, jnp.full(x.shape, i, jnp.int32), axis=0)


def invert_factor(rows, store, hook):
    shape = rows[0].shape
    lane = lax.broadcasted_iota(jnp.int32, shape, 1)
    sub = lax.broadcasted_iota(jnp.int32, shape, 0)
    groups = len(rows)
    for k in range(groups):
        first = ROWS * k
        inside = (lane >= first) & (lane < first + ROWS)
        cols = [from_lane(rows[k], first + i) for i in range(ROWS)]
        piv = {(m, i): from_row(cols[i], m) for i in range(ROWS) for m in range(i, ROWS)}
        panel = jnp.where(inside, jnp.where(lane - first == sub, 1.0, 0.0), rows[k])
        line = [jnp.broadcast_to(panel[i : i + 1, :], shape) for i in range(ROWS)]
        near = range(k + 1, min(k + 1 + NEAR, groups))
        mult = {g: [from_lane(rows[g], first + i) for i in range(ROWS)] for g in near}
        kept = {g: jnp.where(inside, 0.0, rows[g]) for g in near}
        for i in range(ROWS):
            inverse = 1.0 / piv[i, i]
            ratio = {m: piv[m, i] * inverse for m in range(i + 1, ROWS)}
            for m in range(i + 1, ROWS):
                for p in range(i + 1, m + 1):
                    piv[m, p] = piv[m, p] - ratio[m] * piv[p, i]
            for m in range(i + 1, ROWS):
                line[m] = line[m] - ratio[m] * line[i]
            for g in near:
                for p in range(i + 1, ROWS):
                    mult[g][p] = mult[g][p] - mult[g][i] * ratio[p]
                kept[g] = kept[g] - (mult[g][i] * inverse) * line[i]
        for g in near:
            rows[g] = kept[g]
        out = line[0] * lax.rsqrt(piv[0, 0])
        for m in range(1, ROWS):
            out = jnp.where(sub == m, line[m] * lax.rsqrt(piv[m, m]), out)
        if k + 1 + NEAR < groups:
            far = rank_update(out)
            for g in range(k + 1 + NEAR, groups):
                rows[g] = jnp.where(inside, 0.0, rows[g]) - far[ROWS * g : ROWS * g + ROWS, :]
        store(k, jnp.where(lane < first + ROWS, out, 0.0))
        hook(groups - 1 - k)


class Queue:
    def __init__(self):
        self.work = []

    def add(self, task):
        self.work.append(task)

    def some(self, left):
        for _ in range(-(-len(self.work) // (left + 1))):
            self.work.pop(0)()

    def all(self):
        while self.work:
            self.work.pop(0)()


def factorize(a, low, inv, queue, after):
    size = a.shape[0] // PARTS

    def at(i, count=1):
        return slice(i * size, (i + count) * size)

    for k in range(PARTS):
        def store(g, value, k=k):
            inv[k * size + ROWS * g : k * size + ROWS * g + ROWS, :] = value

        rows = [a[k * size + ROWS * g : k * size + ROWS * g + ROWS, at(k)] for g in range(size // ROWS)]
        invert_factor(rows, store, queue.some)
        queue.all()
        if k + 1 < PARTS:
            block = exact(a[at(k + 1), at(k)], inv[at(k), :], NT)
            low[at(k + 1), at(k)] = block
            a[at(k + 1), at(k + 1)] = a[at(k + 1), at(k + 1)] - exact(block, block, NT)
        rest = PARTS - k - 2
        if rest > 0:
            def solve(k=k, rest=rest):
                low[at(k + 2, rest), at(k)] = exact(a[at(k + 2, rest), at(k)], inv[at(k), :], NT)

            queue.add(solve)
            for i in range(k + 1, PARTS):
                def trail(k=k, i=i):
                    j = max(i, k + 2)
                    many = at(j, PARTS - j)
                    a[many, at(i)] = a[many, at(i)] - exact(low[many, at(k)], low[at(i), at(k)], NT)

                queue.add(trail)
        after(k)


def packed_blocks():
    order = []
    for j in range(PARTS):
        if j % 2 == 0:
            order.append(("pair", j))
        order += [("block", i, j) for i in range(j + 1, PARTS)]
    return order


def lower_mask(size):
    row = lax.broadcasted_iota(jnp.int32, (size, size), 0)
    col = lax.broadcasted_iota(jnp.int32, (size, size), 1)
    return row, col


def schur_kernel(rt, proj, diag, rhs, keep, send, full, pack):
    me = lax.axis_index("scen")
    link, share = rt.shape[0], diag.shape[0]
    size = link // PARTS
    for i in range(PARTS):
        upto = (i + 1) * size
        full[i * size : upto, :upto] = dot(rt[i * size : upto, :], rt[:upto, :], NT)
        if i + 1 < PARTS:
            full[i * size : upto, upto:] = jnp.zeros((size, link - upto), F32)
    mine = pl.ds(pl.multiple_of(me * share, ROWS), share)
    full[mine, :] = full[mine, :] + diag[...]
    vec = dot(proj[...].astype(BF16), rt[...], NT) + rhs[...]
    row, col = lower_mask(size)
    order = packed_blocks()
    half = len(order) // 2
    spare = []

    def block(i, j):
        return full[i * size : (i + 1) * size, j * size : (j + 1) * size]

    for n, entry in enumerate(order):
        if entry[0] == "pair":
            j = entry[1]
            second = block(j + 1, j + 1)
            value = jnp.where(row >= col, block(j, j), second)
            spare.append(jnp.sum(jnp.where(row == col, second, 0.0), axis=0, keepdims=True))
        else:
            value = block(entry[1], entry[2])
        pack[n // half, (n % half) * size : (n % half + 1) * size, :] = value
    pack[0, half * size :, :] = jnp.concatenate([vec[:, j * size : (j + 1) * size] for j in range(PARTS)], 0)
    spare.append(jnp.zeros((2 * PARTS - len(spare), size), F32))
    pack[1, half * size :, :] = jnp.concatenate(spare, 0)
    core = lax.rem(me, 2)
    keep[...] = pack[core]
    send[...] = pack[1 - core]


def node_kernel(mine, other, *refs):
    pieces, refs = refs[: refs_pieces(refs)], refs[refs_pieces(refs) :]
    strip, wide, low, inv, wz, a, link_full, acc, sems = refs
    me = lax.axis_index("scen")
    share, link = pieces[0].shape
    size = link // PARTS
    copies = []
    for p, piece in enumerate(pieces):
        start = pl.multiple_of(lax.bitwise_xor(me, p) * share, ROWS)
        copies.append(pltpu.make_async_copy(piece, link_full.at[pl.ds(start, share), :], sems.at[p]))
        copies[-1].start()
    core = lax.rem(me, 2)
    order = packed_blocks()
    half = len(order) // 2
    row, col = lower_mask(size)

    def part(n, r0, r1):
        want = jnp.full((r1 - r0, size), n // half, jnp.int32) == core
        r0, r1 = (n % half) * size + r0, (n % half) * size + r1
        return jnp.where(want, mine[r0:r1, :], other[r0:r1, :])

    def at(i, count=1):
        return slice(i * size, (i + count) * size)

    vec = part(half - 1, size, size + 2 * PARTS)
    spare = part(2 * half - 1, size, size + 2 * PARTS)
    pairs = 0
    for n, entry in enumerate(order):
        if entry[0] == "pair":
            j = entry[1]
            both = part(n, 0, size)
            flip = both.T
            a[at(j), at(j)] = jnp.where(row >= col, both, flip)
            edge = jnp.broadcast_to(spare[pairs : pairs + 1, :], (size, size))
            a[at(j + 1), at(j + 1)] = jnp.where(row == col, edge, jnp.where(row < col, both, flip))
            pairs += 1
        else:
            a[at(entry[1]), at(entry[2])] = part(n, 0, size)
    pad = jnp.zeros((ROWS - 2, size), F32)
    z = [jnp.concatenate([vec[2 * j : 2 * j + 2, :], pad], 0) for j in range(PARTS)]
    for copy in copies:
        copy.wait()
    queue = Queue()
    strip_of = lax.div(me * share, size)
    lanes = [pl.ds(pl.multiple_of(lax.rem(strip_of + PARTS - d, PARTS) * size, size), size) for d in range(3)]
    rz = {0: z[0]}

    def after(k):
        def spread():
            wide[at(k), :] = exact(inv[at(k), :], link_full[at(k), :], NN)

        def vector():
            wz[:, at(k)] = exact(rz[k], inv[at(k), :], NT)

        def products(d):
            def run():
                term = exact(wide[at(k), lanes[0]], wide[at(k), lanes[d]], TN)
                acc[at(d), :] = term if k == 0 else acc[at(d), :] + term
            return run

        def right():
            term = exact(wz[:, at(k)], wide[at(k), lanes[0]], NN)
            acc[3 * size :, :] = term if k == 0 else acc[3 * size :, :] + term

        def coming():
            link_full[at(k + 1), :] = link_full[at(k + 1), :] - exact(low[at(k + 1), at(0, k + 1)], wide[at(0, k + 1), :], NN)
            rz[k + 1] = z[k + 1] - exact(wz[:, at(0, k + 1)], low[at(k + 1), at(0, k + 1)], NT)

        for task in (spread, vector, products(0), products(1), products(2), right):
            queue.add(task)
        if k + 1 < PARTS:
            queue.add(coming)

    factorize(a, low, inv, queue, after)
    queue.all()
    own, above, cross = acc[at(0), :], acc[at(1), :], acc[at(2), :]
    mixed = jnp.where(row >= col, own, cross)
    edge = jnp.sum(jnp.where(row == col, cross, 0.0), axis=0, keepdims=True)
    tail = lax.broadcasted_iota(jnp.int32, (ROWS, size), 0)
    if share == size:
        strip[:share, :] = above
        strip[share : 2 * share, :] = mixed
    else:
        acc[at(0), :] = mixed
        inner = pl.multiple_of(lax.rem(me * share, size), ROWS)
        strip[:share, :] = acc[pl.ds(size + inner, share), :]
        strip[share : 2 * share, :] = acc[pl.ds(inner, share), :]
    strip[2 * share :, :] = jnp.where(tail == 2, jnp.broadcast_to(edge, (ROWS, size)), acc[3 * size :, :])


def refs_pieces(refs):
    return len(refs) - 9


def root_kernel(*refs):
    count = len(refs) - 26
    pieces, refs = refs[:count], refs[count:]
    root_diag, root_rhs, proj, wide_h, low_h, inv_h, wz_h, rt_h, factor_h, leaf, node, root = refs[:12]
    wide, nlow, ninv, nwz, rt, factor, a, low, inv, strips, mixes, ends, whole, sems = refs[12:]
    me = lax.axis_index("scen")
    link = root_diag.shape[0]
    size = link // PARTS
    share = (pieces[0].shape[0] - ROWS) // 2
    copies = []
    for n, (src, dst) in enumerate(((low_h, nlow), (inv_h, ninv), (wide_h, wide), (wz_h, nwz), (rt_h, rt), (factor_h, factor))):
        copies.append(pltpu.make_async_copy(src, dst, sems.at[n]))
        copies[-1].start()

    def at(i, count=1):
        return slice(i * size, (i + count) * size)

    for p, piece in enumerate(pieces):
        who = lax.bitwise_xor(me, p)
        rows = pl.ds(pl.multiple_of(who * share, ROWS), share)
        strips[rows, :] = piece[:share, :]
        mixes[rows, :] = piece[share : 2 * share, :]
        ends[pl.ds(pl.multiple_of(lax.div(who * share, size) * ROWS, ROWS), ROWS), :] = piece[2 * share :, :]
    row, col = lower_mask(size)
    flips = []
    for i in range(PARTS):
        mix = mixes[at(i), :]
        flips.append(mix.T)
        a[at(i), at(i)] = jnp.where(row >= col, mix, flips[i]) + root_diag[at(i), at(i)]
        if i > 0:
            a[at(i), at(i - 1)] = strips[at(i), :] + root_diag[at(i), at(i - 1)]
    a[at(3), at(0)] = strips[at(0), :].T + root_diag[at(3), at(0)]
    for i in (2, 3):
        edge = jnp.broadcast_to(ends[ROWS * i + 2 : ROWS * i + 3, :], (size, size))
        a[at(i), at(i - 2)] = jnp.where(row == col, edge, jnp.where(row < col, mixes[at(i), :], flips[i - 2])) + root_diag[at(i), at(i - 2)]
    pad = jnp.zeros((ROWS - 2, size), F32)
    rhs = [jnp.concatenate([ends[ROWS * i : ROWS * i + 2, :] - root_rhs[:, at(i)], pad], 0) for i in range(PARTS)]
    for copy in copies:
        copy.wait()
    queue = Queue()
    u = {}

    def after(k):
        def forward():
            r = rhs[k]
            for j in range(k):
                r = r - exact(u[j], low[at(k), at(j)], NT)
            u[k] = exact(r, inv[at(k), :], NT)

        queue.add(forward)

    factorize(a, low, inv, queue, after)
    queue.all()
    x = {}
    for k in reversed(range(PARTS)):
        r = u[k]
        for j in range(k + 1, PARTS):
            r = r - exact(x[j], low[at(j), at(k)], NN)
        x[k] = exact(r, inv[at(k), :], NN)
        root[:, at(k)] = x[k][:2, :]
    x0 = jnp.concatenate([x[k] for k in range(PARTS)], 1)
    t = nwz[...] - exact(x0, wide[...], NT)
    xn = {}
    for k in reversed(range(PARTS)):
        r = t[:, at(k)]
        for j in range(k + 1, PARTS):
            r = r - exact(xn[j], nlow[at(j), at(k)], NN)
        xn[k] = exact(r, ninv[at(k), :], NN)
    solved = jnp.concatenate([xn[k] for k in range(PARTS)], 1)
    whole[...] = solved
    if node.shape[1] == size:
        node[...] = whole[:2, pl.ds(pl.multiple_of(me * share, size), size)]
    else:
        node[...] = whole[:2, :]
    update = dot(solved.astype(BF16), rt[...], NN)
    difference = (update[:2, :] - proj[...]).astype(BF16)
    leaf[...] = dot(difference, factor[...], NT)


def swap(x, axis, count, bit):
    return lax.ppermute(x, axis, [(i, i ^ bit) for i in range(count)])


def bits(count, low=1):
    step = low
    while step < count:
        yield step
        step *= 2


def spread(pieces, axis, count, steps):
    for bit in steps:
        for p in list(pieces):
            pieces[p ^ bit] = swap(pieces[p], axis, count, bit)
    return pieces


def build(scen, node):
    vmem = pl.BlockSpec(memory_space=pltpu.VMEM)
    anywhere = pl.BlockSpec(memory_space=pl.ANY)

    def local(factors, couple, leaf_rhs, node_diag, node_rhs, link_root, root_diag, root_rhs):
        factor, coupling, rights = factors[0, 0], couple[0, 0], leaf_rhs[0, 0]
        order, link = coupling.shape
        share = node_diag.shape[1]
        size = link // PARTS
        me = lax.axis_index("scen")
        down = list(reversed(list(bits(scen))))
        links = spread({0: link_root[0]}, "scen", scen, down)
        rt = lax.dot_general(coupling, factor, (TN, ((), ())), preferred_element_type=F32).astype(BF16)
        projected = jnp.dot(rights, factor, preferred_element_type=F32)
        rhs = lax.dynamic_update_slice(jnp.zeros((2, link), F32), node_rhs[0], (0, me * share))
        tall = PARTS * size + 2 * PARTS
        flat = jax.ShapeDtypeStruct((tall, size), F32)
        keep, send = pl.pallas_call(
            schur_kernel,
            out_shape=(flat, flat),
            in_specs=[vmem] * 4,
            out_specs=(vmem, vmem),
            scratch_shapes=[pltpu.VMEM((link, link), F32), pltpu.VMEM((2, tall, size), F32)],
            name="schur",
        )(rt, projected, node_diag[0], rhs)
        mine = keep + swap(send, "scen", scen, 1)
        for bit in bits(scen, 2):
            mine = mine + swap(mine, "scen", scen, bit)
        other = swap(mine, "scen", scen, 1)
        square = jax.ShapeDtypeStruct((link, link), F32)
        strip, wide, low, inv, wz = pl.pallas_call(
            node_kernel,
            out_shape=(
                jax.ShapeDtypeStruct((2 * share + ROWS, size), F32),
                square,
                square,
                jax.ShapeDtypeStruct((link, size), F32),
                jax.ShapeDtypeStruct((ROWS, link), F32),
            ),
            in_specs=[vmem, vmem] + [anywhere] * scen,
            out_specs=(vmem,) * 5,
            scratch_shapes=[
                pltpu.VMEM((link, link), F32),
                pltpu.VMEM((link, link), F32),
                pltpu.VMEM((3 * size + ROWS, size), F32),
                pltpu.SemaphoreType.DMA((scen,)),
            ],
            name="node",
        )(mine, other, *[links[p] for p in range(scen)])
        for bit in bits(node):
            strip = strip + swap(strip, "node", node, bit)
        strips = spread({0: strip}, "scen", scen, down)
        aligned = share % size == 0
        leaf, solved, root = pl.pallas_call(
            root_kernel,
            out_shape=(
                jax.ShapeDtypeStruct((2, order), F32),
                jax.ShapeDtypeStruct((2, share if aligned else link), F32),
                jax.ShapeDtypeStruct((2, link), F32),
            ),
            in_specs=[vmem] * (scen + 3) + [anywhere] * 6,
            out_specs=(vmem,) * 3,
            scratch_shapes=[
                pltpu.VMEM((link, link), F32),
                pltpu.VMEM((link, link), F32),
                pltpu.VMEM((link, size), F32),
                pltpu.VMEM((ROWS, link), F32),
                pltpu.VMEM((link, order), BF16),
                pltpu.VMEM((order, order), BF16),
                pltpu.VMEM((link, link), F32),
                pltpu.VMEM((link, link), F32),
                pltpu.VMEM((link, size), F32),
                pltpu.VMEM((link, size), F32),
                pltpu.VMEM((link, size), F32),
                pltpu.VMEM((PARTS * ROWS, size), F32),
                pltpu.VMEM((ROWS, link), F32),
                pltpu.SemaphoreType.DMA((6,)),
            ],
            name="root",
        )(*[strips[p] for p in range(scen)], root_diag, root_rhs, projected, wide, low, inv, wz, rt, factor)
        if not aligned:
            solved = lax.dynamic_slice(solved, (0, me * share), (2, share))
        return (leaf[None, None], solved[None], root)

    return local


def solution(mesh):
    placed = (
        P("node", "scen", None, None),
        P("node", "scen", None, None),
        P("node", "scen", None, None),
        P("node", "scen", None),
        P("node", None, "scen"),
        P("node", "scen", None),
        P(),
        P(),
    )
    return jax.shard_map(
        build(mesh.shape["scen"], mesh.shape["node"]),
        mesh=mesh,
        in_specs=placed,
        out_specs=(P("node", "scen", None, None), P("node", None, "scen"), P()),
        check_vma=False,
    )
```

```python
import jax
import jax.numpy as jnp
from jax import lax
from jax.experimental import pallas as pl
from jax.experimental.pallas import tpu as pltpu
from jax.sharding import PartitionSpec as P

F32, BF16 = jnp.float32, jnp.bfloat16
NN, NT, TN = ((1,), (0,)), ((1,), (1,)), ((0,), (0,))
ROWS = 8
PARTS = 4
GRANT = 24 << 20
PANEL = 16


def dot(a, b, dims):
    return lax.dot_general(a, b, (dims, ((), ())), preferred_element_type=F32)


def thirds(x):
    high = x.astype(BF16)
    rest = x - high.astype(F32)
    mid = rest.astype(BF16)
    return high, mid, (rest - mid.astype(F32)).astype(BF16)


def exact(a, b, dims):
    (ah, am, al), (bh, bm, bl) = thirds(a), thirds(b)
    left = jnp.concatenate([ah, ah, am, am, ah, al], dims[0][0])
    right = jnp.concatenate([bh, bm, bh, bm, bl, bh], dims[1][0])
    return dot(left, right, dims)


def rank_update(u):
    high = u.astype(BF16).astype(F32)
    rest = u - high
    mid = rest.astype(BF16).astype(F32)
    low = rest - mid
    left = jnp.concatenate([high, high, mid, mid, high, low], 0).astype(BF16)
    right = jnp.concatenate([high, mid, high, mid, low, high], 0).astype(BF16)
    return dot(left, right, TN)


def from_lane(x, i):
    return jnp.broadcast_to(x[:, i : i + 1], x.shape)


def from_row(x, i):
    return jnp.take_along_axis(x, jnp.full(x.shape, i, jnp.int32), axis=0)


def invert_factor(rows, store, hook):
    shape = rows[0].shape
    lane = lax.broadcasted_iota(jnp.int32, shape, 1)
    sub = lax.broadcasted_iota(jnp.int32, shape, 0)
    groups, span = len(rows), PANEL // ROWS
    for k in range(0, groups, span):
        first = ROWS * k
        inside = (lane >= first) & (lane < first + PANEL)
        own = range(k, k + span)
        near = range(k + span, min(k + 2 * span, groups))
        both = [*own, *near]
        cols = {(i, g): from_lane(rows[g], first + i) for i in range(PANEL) for g in both if g >= k + i // ROWS}
        lines = {g: jnp.where(inside, jnp.where(lane - ROWS * g == sub, 1.0, 0.0), rows[g]) for g in own}
        kept = {g: jnp.where(inside, 0.0, rows[g]) for g in near}

        def entry(j, i):
            return from_row(cols[i, k + j // ROWS], j % ROWS)

        pivots = [entry(0, 0)]
        for i in range(PANEL):
            home, at = k + i // ROWS, i % ROWS
            inverse = 1.0 / pivots[i]
            if i + 1 < PANEL:
                below = entry(i + 1, i)
                pivots.append(entry(i + 1, i + 1) - (below * inverse) * below)
            ratio = {g: cols[i, g] * inverse for g in both if g >= home}
            for p in range(i + 1, PANEL):
                across = entry(p, i)
                for g in both:
                    if g >= k + p // ROWS:
                        cols[p, g] = cols[p, g] - ratio[g] * across
            line = jnp.broadcast_to(lines[home][at : at + 1, :], shape)
            for g in own:
                if g > home:
                    lines[g] = lines[g] - ratio[g] * line
                elif g == home and at < ROWS - 1:
                    lines[g] = lines[g] - jnp.where(sub > at, ratio[g], 0.0) * line
            for g in near:
                kept[g] = kept[g] - ratio[g] * line
        for g in near:
            rows[g] = kept[g]
        done = []
        for o in range(span):
            pivot = pivots[ROWS * o]
            for m in range(1, ROWS):
                pivot = jnp.where(sub == m, pivots[ROWS * o + m], pivot)
            done.append(lines[k + o] * lax.rsqrt(pivot))
        if k + 2 * span < groups:
            far = rank_update(jnp.concatenate(done, 0))
            for g in range(k + 2 * span, groups):
                rows[g] = jnp.where(inside, 0.0, rows[g]) - far[ROWS * g : ROWS * g + ROWS, :]
        for o in range(span):
            store(k + o, jnp.where(lane - sub <= ROWS * (k + o), done[o], 0.0))
        hook((groups - k) // span - 1)


class Queue:
    def __init__(self):
        self.work = []

    def add(self, task):
        self.work.append(task)

    def some(self, left):
        for _ in range(-(-len(self.work) // (left + 1))):
            self.work.pop(0)()

    def all(self):
        while self.work:
            self.work.pop(0)()


def factorize(a, low, inv, queue, after):
    size = a.shape[0] // PARTS

    def at(i, count=1):
        return slice(i * size, (i + count) * size)

    for k in range(PARTS):
        def store(g, value, k=k):
            inv[k * size + ROWS * g : k * size + ROWS * g + ROWS, :] = value

        rows = [a[k * size + ROWS * g : k * size + ROWS * g + ROWS, at(k)] for g in range(size // ROWS)]
        invert_factor(rows, store, queue.some)
        queue.all()
        if k + 1 < PARTS:
            block = exact(a[at(k + 1), at(k)], inv[at(k), :], NT)
            low[at(k + 1), at(k)] = block
            a[at(k + 1), at(k + 1)] = a[at(k + 1), at(k + 1)] - exact(block, block, NT)
        rest = PARTS - k - 2
        if rest > 0:
            def solve(k=k, rest=rest):
                low[at(k + 2, rest), at(k)] = exact(a[at(k + 2, rest), at(k)], inv[at(k), :], NT)

            queue.add(solve)
            for i in range(k + 1, PARTS):
                def trail(k=k, i=i):
                    j = max(i, k + 2)
                    many = at(j, PARTS - j)
                    a[many, at(i)] = a[many, at(i)] - exact(low[many, at(k)], low[at(i), at(k)], NT)

                queue.add(trail)
        after(k)


def packed_blocks():
    order = []
    for j in range(PARTS):
        if j % 2 == 0:
            order.append(("pair", j))
        order += [("block", i, j) for i in range(j + 1, PARTS)]
    return order


def lower_mask(size):
    row = lax.broadcasted_iota(jnp.int32, (size, size), 0)
    col = lax.broadcasted_iota(jnp.int32, (size, size), 1)
    return row, col


def schur_kernel(factor_h, couple_h, diag_h, rights_h, rhs_h, rt, proj, keep, send, factor, couple, turned, diag, rights, rhs, full, pack, line, sems):
    me = lax.axis_index("scen")
    order, link = couple.shape
    share = diag.shape[0]
    size = link // PARTS
    width = order // PARTS
    loads = [pltpu.make_async_copy(couple_h, couple, sems.at[PARTS])]
    small = ((rights_h, rights), (diag_h, diag), (rhs_h, rhs))
    small = [pltpu.make_async_copy(src, dst, sems.at[PARTS + 1 + n]) for n, (src, dst) in enumerate(small)]
    for c in range(PARTS):
        cut = slice(c * width, (c + 1) * width)
        loads.append(pltpu.make_async_copy(factor_h.at[:, cut], factor.at[:, cut], sems.at[c]))
    for load in [*loads, *small]:
        load.start()
    loads[0].wait()
    turned[...] = couple[...].T
    for c in range(PARTS):
        cut = slice(c * width, (c + 1) * width)
        loads[1 + c].wait()
        rt[:, cut] = dot(turned[...], factor[:, cut], NN).astype(BF16)
        if c == 0:
            small[0].wait()
        proj[:, cut] = dot(rights[...], factor[:, cut], NN)
        for i in range(PARTS):
            rows, upto = slice(i * size, (i + 1) * size), (i + 1) * size
            term = dot(rt[rows, cut], rt[:upto, cut], NT)
            full[rows, :upto] = term if c == 0 else full[rows, :upto] + term
    small[1].wait()
    small[2].wait()
    for i in range(PARTS - 1):
        full[i * size : (i + 1) * size, (i + 1) * size :] = jnp.zeros((size, link - (i + 1) * size), F32)
    mine = pl.ds(pl.multiple_of(me * share, ROWS), share)
    full[mine, :] = full[mine, :] + diag[...]
    vec = dot(proj[...].astype(BF16), rt[...], NT)
    if rhs.shape[1] == link:
        vec = vec + rhs[...]
    else:
        line[...] = vec
        mine = pl.ds(pl.multiple_of(me * share, size), share)
        line[:, mine] = line[:, mine] + rhs[...]
        vec = line[...]
    row, col = lower_mask(size)
    order = packed_blocks()
    half = len(order) // 2
    spare = []

    def block(i, j):
        return full[i * size : (i + 1) * size, j * size : (j + 1) * size]

    for n, entry in enumerate(order):
        if entry[0] == "pair":
            j = entry[1]
            second = block(j + 1, j + 1)
            value = jnp.where(row >= col, block(j, j), second)
            spare.append(jnp.sum(jnp.where(row == col, second, 0.0), axis=0, keepdims=True))
        else:
            value = block(entry[1], entry[2])
        pack[n // half, (n % half) * size : (n % half + 1) * size, :] = value
    pack[0, half * size :, :] = jnp.concatenate([vec[:, j * size : (j + 1) * size] for j in range(PARTS)], 0)
    spare.append(jnp.zeros((2 * PARTS - len(spare), size), F32))
    pack[1, half * size :, :] = jnp.concatenate(spare, 0)
    core = lax.rem(me, 2)
    keep[...] = pack[core]
    send[...] = pack[1 - core]


def node_kernel(mine, other, *refs):
    pieces, refs = refs[: refs_pieces(refs)], refs[refs_pieces(refs) :]
    strip, wide, low, inv, wz, a, link_full, acc, sems = refs
    me = lax.axis_index("scen")
    share, link = pieces[0].shape
    size = link // PARTS
    copies = []
    for p, piece in enumerate(pieces):
        start = pl.multiple_of(lax.bitwise_xor(me, p) * share, ROWS)
        copies.append(pltpu.make_async_copy(piece, link_full.at[pl.ds(start, share), :], sems.at[p]))
        copies[-1].start()
    core = lax.rem(me, 2)
    order = packed_blocks()
    half = len(order) // 2
    row, col = lower_mask(size)

    def part(n, r0, r1):
        want = jnp.full((r1 - r0, size), n // half, jnp.int32) == core
        r0, r1 = (n % half) * size + r0, (n % half) * size + r1
        return jnp.where(want, mine[r0:r1, :], other[r0:r1, :])

    def at(i, count=1):
        return slice(i * size, (i + count) * size)

    vec = part(half - 1, size, size + 2 * PARTS)
    spare = part(2 * half - 1, size, size + 2 * PARTS)
    pairs = 0
    for n, entry in enumerate(order):
        if entry[0] == "pair":
            j = entry[1]
            both = part(n, 0, size)
            flip = both.T
            a[at(j), at(j)] = jnp.where(row >= col, both, flip)
            edge = jnp.broadcast_to(spare[pairs : pairs + 1, :], (size, size))
            a[at(j + 1), at(j + 1)] = jnp.where(row == col, edge, jnp.where(row < col, both, flip))
            pairs += 1
        else:
            a[at(entry[1]), at(entry[2])] = part(n, 0, size)
    pad = jnp.zeros((ROWS - 2, size), F32)
    z = [jnp.concatenate([vec[2 * j : 2 * j + 2, :], pad], 0) for j in range(PARTS)]
    for copy in copies:
        copy.wait()
    queue = Queue()
    strip_of = lax.div(me * share, size)
    lanes = [pl.ds(pl.multiple_of(lax.rem(strip_of + PARTS - d, PARTS) * size, size), size) for d in range(3)]
    rz = {0: z[0]}

    def after(k):
        def spread():
            wide[at(k), :] = exact(inv[at(k), :], link_full[at(k), :], NN)

        def vector():
            wz[:, at(k)] = exact(rz[k], inv[at(k), :], NT)

        def products(d):
            def run():
                term = exact(wide[at(k), lanes[0]], wide[at(k), lanes[d]], TN)
                acc[at(d), :] = term if k == 0 else acc[at(d), :] + term
            return run

        def right():
            term = exact(wz[:, at(k)], wide[at(k), lanes[0]], NN)
            acc[3 * size :, :] = term if k == 0 else acc[3 * size :, :] + term

        def coming():
            link_full[at(k + 1), :] = link_full[at(k + 1), :] - exact(low[at(k + 1), at(0, k + 1)], wide[at(0, k + 1), :], NN)
            rz[k + 1] = z[k + 1] - exact(wz[:, at(0, k + 1)], low[at(k + 1), at(0, k + 1)], NT)

        for task in (spread, vector, products(0), products(1), products(2), right):
            queue.add(task)
        if k + 1 < PARTS:
            queue.add(coming)

    factorize(a, low, inv, queue, after)
    queue.all()
    own, above, cross = acc[at(0), :], acc[at(1), :], acc[at(2), :]
    mixed = jnp.where(row >= col, own, cross)
    edge = jnp.sum(jnp.where(row == col, cross, 0.0), axis=0, keepdims=True)
    tail = lax.broadcasted_iota(jnp.int32, (ROWS, size), 0)
    if share == size:
        strip[:share, :] = above
        strip[share : 2 * share, :] = mixed
    else:
        acc[at(0), :] = mixed
        inner = pl.multiple_of(lax.rem(me * share, size), ROWS)
        strip[:share, :] = acc[pl.ds(size + inner, share), :]
        strip[share : 2 * share, :] = acc[pl.ds(inner, share), :]
    strip[2 * share :, :] = jnp.where(tail == 2, jnp.broadcast_to(edge, (ROWS, size)), acc[3 * size :, :])


def refs_pieces(refs):
    return len(refs) - 9


def root_kernel(*refs):
    count = len(refs) - 26
    pieces, refs = refs[:count], refs[count:]
    root_diag, root_rhs, proj, wide_h, low_h, inv_h, wz_h, rt_h, factor_h, leaf, node, root = refs[:12]
    wide, nlow, ninv, nwz, rt, factor, a, low, inv, strips, mixes, ends, whole, sems = refs[12:]
    me = lax.axis_index("scen")
    link = root_diag.shape[0]
    size = link // PARTS
    share = (pieces[0].shape[0] - ROWS) // 2
    copies = []
    for n, (src, dst) in enumerate(((low_h, nlow), (inv_h, ninv), (wide_h, wide), (wz_h, nwz), (rt_h, rt), (factor_h, factor))):
        copies.append(pltpu.make_async_copy(src, dst, sems.at[n]))
        copies[-1].start()

    def at(i, count=1):
        return slice(i * size, (i + count) * size)

    for p, piece in enumerate(pieces):
        who = lax.bitwise_xor(me, p)
        rows = pl.ds(pl.multiple_of(who * share, ROWS), share)
        strips[rows, :] = piece[:share, :]
        mixes[rows, :] = piece[share : 2 * share, :]
        ends[pl.ds(pl.multiple_of(lax.div(who * share, size) * ROWS, ROWS), ROWS), :] = piece[2 * share :, :]
    row, col = lower_mask(size)
    flips = []
    for i in range(PARTS):
        mix = mixes[at(i), :]
        flips.append(mix.T)
        a[at(i), at(i)] = jnp.where(row >= col, mix, flips[i]) + root_diag[at(i), at(i)]
        if i > 0:
            a[at(i), at(i - 1)] = strips[at(i), :] + root_diag[at(i), at(i - 1)]
    a[at(3), at(0)] = strips[at(0), :].T + root_diag[at(3), at(0)]
    for i in (2, 3):
        edge = jnp.broadcast_to(ends[ROWS * i + 2 : ROWS * i + 3, :], (size, size))
        a[at(i), at(i - 2)] = jnp.where(row == col, edge, jnp.where(row < col, mixes[at(i), :], flips[i - 2])) + root_diag[at(i), at(i - 2)]
    pad = jnp.zeros((ROWS - 2, size), F32)
    rhs = [jnp.concatenate([ends[ROWS * i : ROWS * i + 2, :] - root_rhs[:, at(i)], pad], 0) for i in range(PARTS)]
    for copy in copies:
        copy.wait()
    queue = Queue()
    u = {}

    def after(k):
        def forward():
            r = rhs[k]
            for j in range(k):
                r = r - exact(u[j], low[at(k), at(j)], NT)
            u[k] = exact(r, inv[at(k), :], NT)

        queue.add(forward)

    factorize(a, low, inv, queue, after)
    queue.all()
    x = {}
    for k in reversed(range(PARTS)):
        r = u[k]
        for j in range(k + 1, PARTS):
            r = r - exact(x[j], low[at(j), at(k)], NN)
        x[k] = exact(r, inv[at(k), :], NN)
        root[:, at(k)] = x[k][:2, :]
    x0 = jnp.concatenate([x[k] for k in range(PARTS)], 1)
    t = nwz[...] - exact(x0, wide[...], NT)
    xn = {}
    for k in reversed(range(PARTS)):
        r = t[:, at(k)]
        for j in range(k + 1, PARTS):
            r = r - exact(xn[j], nlow[at(j), at(k)], NN)
        xn[k] = exact(r, ninv[at(k), :], NN)
    solved = jnp.concatenate([xn[k] for k in range(PARTS)], 1)
    whole[...] = solved
    if node.shape[1] == size:
        node[...] = whole[:2, pl.ds(pl.multiple_of(me * share, size), size)]
    else:
        node[...] = whole[:2, :]
    update = dot(solved.astype(BF16), rt[...], NN)
    difference = (update[:2, :] - proj[...]).astype(BF16)
    leaf[...] = dot(difference, factor[...], NT)


def swap(x, axis, count, bit):
    return lax.ppermute(x, axis, [(i, i ^ bit) for i in range(count)])


def bits(count, low=1):
    step = low
    while step < count:
        yield step
        step *= 2


def spread(pieces, axis, count, steps):
    for bit in steps:
        for p in list(pieces):
            pieces[p ^ bit] = swap(pieces[p], axis, count, bit)
    return pieces


def hbm(x):
    return pltpu.with_memory_space_constraint(x, pltpu.HBM)


def build(scen, node):
    vmem = pl.BlockSpec(memory_space=pltpu.VMEM)
    anywhere = pl.BlockSpec(memory_space=pl.ANY)
    far = pl.BlockSpec(memory_space=pltpu.HBM)

    def local(factors, couple, leaf_rhs, node_diag, node_rhs, link_root, root_diag, root_rhs):
        factor, coupling, rights = factors[0, 0], couple[0, 0], leaf_rhs[0, 0]
        order, link = coupling.shape
        share = node_diag.shape[1]
        size = link // PARTS
        me = lax.axis_index("scen")
        down = list(reversed(list(bits(scen))))
        links = spread({0: link_root[0]}, "scen", scen, down[:-1])
        rhs = node_rhs[0]
        if share % size:
            rhs = lax.dynamic_update_slice(jnp.zeros((2, link), F32), rhs, (0, me * share))
        tall = PARTS * size + 2 * PARTS
        flat = jax.ShapeDtypeStruct((tall, size), F32)
        rt, projected, keep, send = pl.pallas_call(
            schur_kernel,
            out_shape=(
                jax.ShapeDtypeStruct((link, order), BF16),
                jax.ShapeDtypeStruct((2, order), F32),
                flat,
                flat,
            ),
            in_specs=[far] * 5,
            out_specs=(vmem,) * 4,
            scratch_shapes=[
                pltpu.VMEM((order, order), BF16),
                pltpu.VMEM((order, link), BF16),
                pltpu.VMEM((link, order), BF16),
                pltpu.VMEM((share, link), F32),
                pltpu.VMEM((2, order), BF16),
                pltpu.VMEM(rhs.shape, F32),
                pltpu.VMEM((link, link), F32),
                pltpu.VMEM((2, tall, size), F32),
                pltpu.VMEM((2, link), F32),
                pltpu.SemaphoreType.DMA((PARTS + 4,)),
            ],
            name="schur",
            compiler_params=pltpu.CompilerParams(vmem_limit_bytes=GRANT),
        )(*[hbm(x) for x in (factor, coupling, node_diag[0], rights, rhs)])
        send, links = lax.optimization_barrier((send, links))
        links = spread(links, "scen", scen, down[-1:])
        mine = keep + swap(send, "scen", scen, 1)
        for bit in bits(scen, 2):
            mine = mine + swap(mine, "scen", scen, bit)
        other = swap(mine, "scen", scen, 1)
        square = jax.ShapeDtypeStruct((link, link), F32)
        strip, wide, low, inv, wz = pl.pallas_call(
            node_kernel,
            out_shape=(
                jax.ShapeDtypeStruct((2 * share + ROWS, size), F32),
                square,
                square,
                jax.ShapeDtypeStruct((link, size), F32),
                jax.ShapeDtypeStruct((ROWS, link), F32),
            ),
            in_specs=[vmem, vmem] + [anywhere] * scen,
            out_specs=(vmem,) * 5,
            scratch_shapes=[
                pltpu.VMEM((link, link), F32),
                pltpu.VMEM((link, link), F32),
                pltpu.VMEM((3 * size + ROWS, size), F32),
                pltpu.SemaphoreType.DMA((scen,)),
            ],
            name="node",
            compiler_params=pltpu.CompilerParams(vmem_limit_bytes=GRANT),
        )(mine, other, *[links[p] for p in range(scen)])
        for bit in bits(node):
            strip = strip + swap(strip, "node", node, bit)
        strips = spread({0: strip}, "scen", scen, down)
        aligned = share % size == 0
        leaf, solved, root = pl.pallas_call(
            root_kernel,
            out_shape=(
                jax.ShapeDtypeStruct((2, order), F32),
                jax.ShapeDtypeStruct((2, share if aligned else link), F32),
                jax.ShapeDtypeStruct((2, link), F32),
            ),
            in_specs=[vmem] * (scen + 3) + [anywhere] * 6,
            out_specs=(vmem,) * 3,
            scratch_shapes=[
                pltpu.VMEM((link, link), F32),
                pltpu.VMEM((link, link), F32),
                pltpu.VMEM((link, size), F32),
                pltpu.VMEM((ROWS, link), F32),
                pltpu.VMEM((link, order), BF16),
                pltpu.VMEM((order, order), BF16),
                pltpu.VMEM((link, link), F32),
                pltpu.VMEM((link, link), F32),
                pltpu.VMEM((link, size), F32),
                pltpu.VMEM((link, size), F32),
                pltpu.VMEM((link, size), F32),
                pltpu.VMEM((PARTS * ROWS, size), F32),
                pltpu.VMEM((ROWS, link), F32),
                pltpu.SemaphoreType.DMA((6,)),
            ],
            name="root",
            compiler_params=pltpu.CompilerParams(vmem_limit_bytes=GRANT),
        )(*[strips[p] for p in range(scen)], root_diag, root_rhs, projected, wide, low, inv, wz, rt, factor)
        if not aligned:
            solved = lax.dynamic_slice(solved, (0, me * share), (2, share))
        return (leaf[None, None], solved[None], root)

    return local


def solution(mesh):
    placed = (
        P("node", "scen", None, None),
        P("node", "scen", None, None),
        P("node", "scen", None, None),
        P("node", "scen", None),
        P("node", None, "scen"),
        P("node", "scen", None),
        P(),
        P(),
    )
    return jax.shard_map(
        build(mesh.shape["scen"], mesh.shape["node"]),
        mesh=mesh,
        in_specs=placed,
        out_specs=(P("node", "scen", None, None), P("node", None, "scen"), P()),
        check_vma=False,
    )
```

```python
import jax
import jax.numpy as jnp
from jax import lax
from jax.experimental import pallas as pl
from jax.experimental.pallas import tpu as pltpu
from jax.sharding import PartitionSpec as P


F32, BF16 = jnp.float32, jnp.bfloat16
NN, NT, TN = ((1,), (0,)), ((1,), (1,)), ((0,), (0,))
ROWS = 8
PARTS = 4
GRANT = 24 << 20
PANEL = 16


def dot(a, b, dims):
    return lax.dot_general(a, b, (dims, ((), ())), preferred_element_type=F32)


def thirds(x):
    high = x.astype(BF16)
    rest = x - high.astype(F32)
    mid = rest.astype(BF16)
    return high, mid, (rest - mid.astype(F32)).astype(BF16)


def exact(a, b, dims):
    (ah, am, al), (bh, bm, bl) = thirds(a), thirds(b)
    left = jnp.concatenate([ah, ah, am, am, ah, al], dims[0][0])
    right = jnp.concatenate([bh, bm, bh, bm, bl, bh], dims[1][0])
    return dot(left, right, dims)


def rank_update(u):
    high = u.astype(BF16).astype(F32)
    rest = u - high
    mid = rest.astype(BF16).astype(F32)
    low = rest - mid
    left = jnp.concatenate([high, high, mid, mid, high, low], 0).astype(BF16)
    right = jnp.concatenate([high, mid, high, mid, low, high], 0).astype(BF16)
    return dot(left, right, TN)


def from_lane(x, i):
    return jnp.broadcast_to(x[:, i : i + 1], x.shape)


def from_row(x, i):
    return jnp.take_along_axis(x, jnp.full(x.shape, i, jnp.int32), axis=0)


def invert_factor(rows, store, hook):
    shape = rows[0].shape
    lane = lax.broadcasted_iota(jnp.int32, shape, 1)
    sub = lax.broadcasted_iota(jnp.int32, shape, 0)
    groups, span = len(rows), PANEL // ROWS
    for k in range(0, groups, span):
        first = ROWS * k
        inside = (lane >= first) & (lane < first + PANEL)
        own = range(k, k + span)
        near = range(k + span, min(k + 2 * span, groups))
        both = [*own, *near]
        cols = {(i, g): from_lane(rows[g], first + i) for i in range(PANEL) for g in both if g >= k + i // ROWS}
        lines = {g: jnp.where(inside, jnp.where(lane - ROWS * g == sub, 1.0, 0.0), rows[g]) for g in own}
        kept = {g: jnp.where(inside, 0.0, rows[g]) for g in near}

        def entry(j, i):
            return from_row(cols[i, k + j // ROWS], j % ROWS)

        pivots = [entry(0, 0)]
        for i in range(PANEL):
            home, at = k + i // ROWS, i % ROWS
            inverse = 1.0 / pivots[i]
            if i + 1 < PANEL:
                below = entry(i + 1, i)
                pivots.append(entry(i + 1, i + 1) - (below * inverse) * below)
            ratio = {g: cols[i, g] * inverse for g in both if g >= home}
            for p in range(i + 1, PANEL):
                across = entry(p, i)
                for g in both:
                    if g >= k + p // ROWS:
                        cols[p, g] = cols[p, g] - ratio[g] * across
            line = jnp.broadcast_to(lines[home][at : at + 1, :], shape)
            for g in own:
                if g > home:
                    lines[g] = lines[g] - ratio[g] * line
                elif g == home and at < ROWS - 1:
                    lines[g] = lines[g] - jnp.where(sub > at, ratio[g], 0.0) * line
            for g in near:
                kept[g] = kept[g] - ratio[g] * line
        for g in near:
            rows[g] = kept[g]
        done = []
        for o in range(span):
            pivot = pivots[ROWS * o]
            for m in range(1, ROWS):
                pivot = jnp.where(sub == m, pivots[ROWS * o + m], pivot)
            done.append(lines[k + o] * lax.rsqrt(pivot))
        if k + 2 * span < groups:
            far = rank_update(jnp.concatenate(done, 0))
            for g in range(k + 2 * span, groups):
                rows[g] = jnp.where(inside, 0.0, rows[g]) - far[ROWS * g : ROWS * g + ROWS, :]
        for o in range(span):
            store(k + o, jnp.where(lane - sub <= ROWS * (k + o), done[o], 0.0))
        hook((groups - k) // span - 1)


class Queue:
    def __init__(self):
        self.work = []

    def add(self, task):
        self.work.append(task)

    def some(self, left):
        for _ in range(-(-len(self.work) // (left + 1))):
            self.work.pop(0)()

    def all(self):
        while self.work:
            self.work.pop(0)()


def factorize(a, low, inv, queue, after, known=0):
    size = a.shape[0] // PARTS

    def at(i, count=1):
        return slice(i * size, (i + count) * size)

    for k in range(PARTS):
        def store(g, value, k=k):
            inv[k * size + ROWS * g : k * size + ROWS * g + ROWS, :] = value

        if k >= known:
            rows = [a[k * size + ROWS * g : k * size + ROWS * g + ROWS, at(k)] for g in range(size // ROWS)]
            invert_factor(rows, store, queue.some)
            queue.all()
        if k + 1 < PARTS:
            if k >= known:
                low[at(k + 1), at(k)] = exact(a[at(k + 1), at(k)], inv[at(k), :], NT)
            block = low[at(k + 1), at(k)]
            a[at(k + 1), at(k + 1)] = a[at(k + 1), at(k + 1)] - exact(block, block, NT)
        rest = PARTS - k - 2
        if rest > 0:
            def solve(k=k, rest=rest):
                low[at(k + 2, rest), at(k)] = exact(a[at(k + 2, rest), at(k)], inv[at(k), :], NT)

            queue.add(solve)
            for i in range(k + 1, PARTS):
                def trail(k=k, i=i):
                    j = max(i, k + 2)
                    many = at(j, PARTS - j)
                    a[many, at(i)] = a[many, at(i)] - exact(low[many, at(k)], low[at(i), at(k)], NT)

                queue.add(trail)
        after(k)


FIRST = (((0, 0),), ((1, 0),))
REST = (((2, 0), (3, 0), (2, 1)), ((3, 1), (2, 2), (3, 2)))


def lower_mask(size):
    row = lax.broadcasted_iota(jnp.int32, (size, size), 0)
    col = lax.broadcasted_iota(jnp.int32, (size, size), 1)
    return row, col


def schur_kernel(factor_h, couple_h, diag_h, rights_h, rhs_h, rt, proj, keep_a, send_a, keep_b, send_b, factor, couple, diag, rights, rhs, full, first, rest, line, sems):
    me = lax.axis_index("scen")
    order, link = couple.shape
    share = diag.shape[0]
    size = link // PARTS
    width = order // 2
    loads = [pltpu.make_async_copy(couple_h, couple, sems.at[0])]
    small = ((rights_h, rights), (diag_h, diag), (rhs_h, rhs))
    small = [pltpu.make_async_copy(src, dst, sems.at[3 + n]) for n, (src, dst) in enumerate(small)]
    for c in range(2):
        cut = slice(c * width, (c + 1) * width)
        loads.append(pltpu.make_async_copy(factor_h.at[:, cut], factor.at[:, cut], sems.at[1 + c]))
    for load in [*loads, *small]:
        load.start()
    loads[0].wait()
    for c in range(2):
        cut = slice(c * width, (c + 1) * width)
        loads[1 + c].wait()
        rt[:, cut] = dot(couple[...], factor[:, cut], TN).astype(BF16)
        if c == 0:
            small[0].wait()
        proj[:, cut] = dot(rights[...], factor[:, cut], NN)
        for i in range(PARTS):
            rows, upto = slice(i * size, (i + 1) * size), (i + 1) * size
            term = dot(rt[rows, cut], rt[:upto, cut], NT)
            full[rows, :upto] = term if c == 0 else full[rows, :upto] + term
    small[1].wait()
    small[2].wait()
    for i in range(PARTS - 1):
        full[i * size : (i + 1) * size, (i + 1) * size :] = jnp.zeros((size, link - (i + 1) * size), F32)
    mine = pl.ds(pl.multiple_of(me * share, ROWS), share)
    full[mine, :] = full[mine, :] + diag[...]
    vec = dot(proj[...].astype(BF16), rt[...], NT)
    if rhs.shape[1] == link:
        vec = vec + rhs[...]
    else:
        line[...] = vec
        mine = pl.ds(pl.multiple_of(me * share, size), share)
        line[:, mine] = line[:, mine] + rhs[...]
        vec = line[...]
    row, col = lower_mask(size)
    spare = []

    def block(i, j):
        return full[i * size : (i + 1) * size, j * size : (j + 1) * size]

    core = lax.rem(me, 2)
    for pack, halves in ((first, FIRST), (rest, REST)):
        for h, entries in enumerate(halves):
            for n, (i, j) in enumerate(entries):
                value = block(i, j)
                if i == j:
                    second = block(j + 1, j + 1)
                    value = jnp.where(row >= col, value, second)
                    spare.append(jnp.sum(jnp.where(row == col, second, 0.0), axis=0, keepdims=True))
                pack[h, n * size : (n + 1) * size, :] = value
    tail = len(REST[0]) * size
    rest[0, tail:, :] = jnp.concatenate([vec[:, j * size : (j + 1) * size] for j in range(PARTS)], 0)
    spare.append(jnp.zeros((2 * PARTS - len(spare), size), F32))
    rest[1, tail:, :] = jnp.concatenate(spare, 0)
    for pack, keep, send in ((first, keep_a, send_a), (rest, keep_b, send_b)):
        keep[...] = pack[core]
        send[...] = pack[1 - core]


def halves_of(mine, other, entries, size):
    core = lax.rem(lax.axis_index("scen"), 2)

    def read(h, r0, r1):
        want = jnp.full((r1 - r0, size), h, jnp.int32) == core
        return jnp.where(want, mine[r0:r1, :], other[r0:r1, :])

    def block(i, j):
        h = 0 if (i, j) in entries[0] else 1
        n = entries[h].index((i, j))
        return read(h, n * size, (n + 1) * size)

    return read, block


def head_kernel(mine, other, inv, under):
    size = inv.shape[0]
    _, block = halves_of(mine, other, FIRST, size)
    row, col = lower_mask(size)
    both = block(0, 0)
    whole = jnp.where(row >= col, both, both.T)
    rows = [whole[ROWS * g : ROWS * g + ROWS, :] for g in range(size // ROWS)]

    def store(g, value):
        inv[ROWS * g : ROWS * g + ROWS, :] = value

    invert_factor(rows, store, lambda left: None)
    under[...] = exact(block(1, 0), inv[...], NT)


def node_kernel(mine_a, other_a, mine_b, other_b, inv_a, under, *refs):
    pieces, refs = refs[: refs_pieces(refs)], refs[refs_pieces(refs) :]
    strip, wide, low, inv, wz, a, link_full, acc, sems = refs
    me = lax.axis_index("scen")
    share, link = pieces[0].shape
    size = link // PARTS
    copies = []
    for p, piece in enumerate(pieces):
        start = pl.multiple_of(lax.bitwise_xor(me, p) * share, ROWS)
        copies.append(pltpu.make_async_copy(piece, link_full.at[pl.ds(start, share), :], sems.at[p]))
        copies[-1].start()
    row, col = lower_mask(size)
    _, block_a = halves_of(mine_a, other_a, FIRST, size)
    read_b, block_b = halves_of(mine_b, other_b, REST, size)

    def at(i, count=1):
        return slice(i * size, (i + count) * size)

    tail = len(REST[0]) * size
    vec, spare = read_b(0, tail, tail + 2 * PARTS), read_b(1, tail, tail + 2 * PARTS)
    inv[at(0), :] = inv_a[...]
    low[at(1), at(0)] = under[...]
    for n, block in enumerate((block_a, block_b)):
        both, edge = block(2 * n, 2 * n), jnp.broadcast_to(spare[n : n + 1, :], (size, size))
        flip = both.T
        if n > 0:
            a[at(2 * n), at(2 * n)] = jnp.where(row >= col, both, flip)
        a[at(2 * n + 1), at(2 * n + 1)] = jnp.where(row == col, edge, jnp.where(row < col, both, flip))
    for i, j in (*REST[0], *REST[1]):
        if i > j:
            a[at(i), at(j)] = block_b(i, j)
    pad = jnp.zeros((ROWS - 2, size), F32)
    z = [jnp.concatenate([vec[2 * j : 2 * j + 2, :], pad], 0) for j in range(PARTS)]
    queue = Queue()
    strip_of = lax.div(me * share, size)
    lanes = [pl.ds(pl.multiple_of(lax.rem(strip_of + PARTS - d, PARTS) * size, size), size) for d in range(3)]
    rz = {0: z[0]}

    def after(k):
        def spread():
            if k == 0:
                for copy in copies:
                    copy.wait()
            wide[at(k), :] = exact(inv[at(k), :], link_full[at(k), :], NN)

        def vector():
            wz[:, at(k)] = exact(rz[k], inv[at(k), :], NT)

        def products(d):
            def run():
                term = exact(wide[at(k), lanes[0]], wide[at(k), lanes[d]], TN)
                acc[at(d), :] = term if k == 0 else acc[at(d), :] + term

            return run

        def right():
            term = exact(wz[:, at(k)], wide[at(k), lanes[0]], NN)
            acc[3 * size :, :] = term if k == 0 else acc[3 * size :, :] + term

        def coming():
            link_full[at(k + 1), :] = link_full[at(k + 1), :] - exact(low[at(k + 1), at(0, k + 1)], wide[at(0, k + 1), :], NN)
            rz[k + 1] = z[k + 1] - exact(wz[:, at(0, k + 1)], low[at(k + 1), at(0, k + 1)], NT)

        for task in (spread, vector, products(0), products(1), products(2), right):
            queue.add(task)
        if k + 1 < PARTS:
            queue.add(coming)

    factorize(a, low, inv, queue, after, 1)
    queue.all()
    own, above, cross = acc[at(0), :], acc[at(1), :], acc[at(2), :]
    mixed = jnp.where(row >= col, own, cross)
    edge = jnp.sum(jnp.where(row == col, cross, 0.0), axis=0, keepdims=True)
    tail = lax.broadcasted_iota(jnp.int32, (ROWS, size), 0)
    if share == size:
        strip[:share, :] = above
        strip[share : 2 * share, :] = mixed
    else:
        acc[at(0), :] = mixed
        inner = pl.multiple_of(lax.rem(me * share, size), ROWS)
        strip[:share, :] = acc[pl.ds(size + inner, share), :]
        strip[share : 2 * share, :] = acc[pl.ds(inner, share), :]
    strip[2 * share :, :] = jnp.where(tail == 2, jnp.broadcast_to(edge, (ROWS, size)), acc[3 * size :, :])


def refs_pieces(refs):
    return len(refs) - 9


def root_kernel(*refs):
    count = len(refs) - 19
    pieces, refs = refs[:count], refs[count:]
    root_diag, root_rhs, proj, wide, nlow, ninv, nwz, rt, factor, leaf, node, root = refs[:12]
    a, low, inv, strips, mixes, ends, whole = refs[12:]
    me = lax.axis_index("scen")
    link = root_diag.shape[0]
    size = link // PARTS
    share = (pieces[0].shape[0] - ROWS) // 2

    def at(i, count=1):
        return slice(i * size, (i + count) * size)

    for p, piece in enumerate(pieces):
        who = lax.bitwise_xor(me, p)
        rows = pl.ds(pl.multiple_of(who * share, ROWS), share)
        strips[rows, :] = piece[:share, :]
        mixes[rows, :] = piece[share : 2 * share, :]
        ends[pl.ds(pl.multiple_of(lax.div(who * share, size) * ROWS, ROWS), ROWS), :] = piece[2 * share :, :]
    row, col = lower_mask(size)
    flips = []
    for i in range(PARTS):
        mix = mixes[at(i), :]
        flips.append(mix.T)
        a[at(i), at(i)] = jnp.where(row >= col, mix, flips[i]) + root_diag[at(i), at(i)]
        if i > 0:
            a[at(i), at(i - 1)] = strips[at(i), :] + root_diag[at(i), at(i - 1)]
    a[at(3), at(0)] = strips[at(0), :].T + root_diag[at(3), at(0)]
    for i in (2, 3):
        edge = jnp.broadcast_to(ends[ROWS * i + 2 : ROWS * i + 3, :], (size, size))
        a[at(i), at(i - 2)] = jnp.where(row == col, edge, jnp.where(row < col, mixes[at(i), :], flips[i - 2])) + root_diag[at(i), at(i - 2)]
    pad = jnp.zeros((ROWS - 2, size), F32)
    rhs = [jnp.concatenate([ends[ROWS * i : ROWS * i + 2, :] - root_rhs[:, at(i)], pad], 0) for i in range(PARTS)]
    queue = Queue()
    u = {}

    def after(k):
        def forward():
            r = rhs[k]
            for j in range(k):
                r = r - exact(u[j], low[at(k), at(j)], NT)
            u[k] = exact(r, inv[at(k), :], NT)

        queue.add(forward)

    factorize(a, low, inv, queue, after)
    queue.all()
    x = {}
    for k in reversed(range(PARTS)):
        r = u[k]
        for j in range(k + 1, PARTS):
            r = r - exact(x[j], low[at(j), at(k)], NN)
        x[k] = exact(r, inv[at(k), :], NN)
        root[:, at(k)] = x[k][:2, :]
    x0 = jnp.concatenate([x[k] for k in range(PARTS)], 1)
    t = nwz[...] - exact(x0, wide[...], NT)
    xn = {}
    for k in reversed(range(PARTS)):
        r = t[:, at(k)]
        for j in range(k + 1, PARTS):
            r = r - exact(xn[j], nlow[at(j), at(k)], NN)
        xn[k] = exact(r, ninv[at(k), :], NN)
    solved = jnp.concatenate([xn[k] for k in range(PARTS)], 1)
    whole[...] = solved
    if node.shape[1] == size:
        node[...] = whole[:2, pl.ds(pl.multiple_of(me * share, size), size)]
    else:
        node[...] = whole[:2, :]
    update = dot(solved.astype(BF16), rt[...], NN)
    difference = (update[:2, :] - proj[...]).astype(BF16)
    leaf[...] = dot(difference, factor[...], NT)


def swap(x, axis, count, bit):
    return lax.ppermute(x, axis, [(i, i ^ bit) for i in range(count)])


def bits(count, low=1):
    step = low
    while step < count:
        yield step
        step *= 2


def spread(pieces, axis, count, steps):
    for bit in steps:
        for p in list(pieces):
            pieces[p ^ bit] = swap(pieces[p], axis, count, bit)
    return pieces


def hbm(x):
    return pltpu.with_memory_space_constraint(x, pltpu.HBM)


def build(scen, node):
    vmem = pl.BlockSpec(memory_space=pltpu.VMEM)
    anywhere = pl.BlockSpec(memory_space=pl.ANY)
    far = pl.BlockSpec(memory_space=pltpu.HBM)

    def run(factors, couple, leaf_rhs, node_diag, node_rhs, link_root, root_diag, root_rhs):
        factor, coupling, rights = factors[0, 0], couple[0, 0], leaf_rhs[0, 0]
        order, link = coupling.shape
        share = node_diag.shape[1]
        size = link // PARTS
        me = lax.axis_index("scen")
        down = list(reversed(list(bits(scen))))
        links = spread({0: link_root[0]}, "scen", scen, down[:-1])
        rhs = node_rhs[0]
        if share % size:
            rhs = lax.dynamic_update_slice(jnp.zeros((2, link), F32), rhs, (0, me * share))
        tall = len(REST[0]) * size + 2 * PARTS
        flat_a, flat_b = (jax.ShapeDtypeStruct((n, size), F32) for n in (size, tall))
        rt, projected, keep_a, send_a, keep_b, send_b = pl.pallas_call(
            schur_kernel,
            out_shape=(
                jax.ShapeDtypeStruct((link, order), BF16),
                jax.ShapeDtypeStruct((2, order), F32),
                flat_a,
                flat_a,
                flat_b,
                flat_b,
            ),
            in_specs=[far] * 5,
            out_specs=(vmem,) * 6,
            scratch_shapes=[
                pltpu.VMEM((order, order), BF16),
                pltpu.VMEM((order, link), BF16),
                pltpu.VMEM((share, link), F32),
                pltpu.VMEM((2, order), BF16),
                pltpu.VMEM(rhs.shape, F32),
                pltpu.VMEM((link, link), F32),
                pltpu.VMEM((2, size, size), F32),
                pltpu.VMEM((2, tall, size), F32),
                pltpu.VMEM((2, link), F32),
                pltpu.SemaphoreType.DMA((6,)),
            ],
            name="schur",
            compiler_params=pltpu.CompilerParams(vmem_limit_bytes=GRANT),
        )(*[hbm(x) for x in (factor, coupling, node_diag[0], rights, rhs)])
        mine_a = keep_a + swap(send_a, "scen", scen, 1)
        mine_b = keep_b + swap(send_b, "scen", scen, 1)
        mine_a, links = lax.optimization_barrier((mine_a, links))
        back = []
        if scen > 2:
            for value in (mine_a, mine_b):
                back.append(swap(value, "scen", scen, 2))
        links = spread(links, "scen", scen, down[-1:])
        if back:
            mine_a = mine_a + back[0]
        for bit in bits(scen, 4):
            mine_a = mine_a + swap(mine_a, "scen", scen, bit)
        other_a = swap(mine_a, "scen", scen, 1)
        corner = jax.ShapeDtypeStruct((size, size), F32)
        inv_a, under = pl.pallas_call(
            head_kernel,
            out_shape=(corner, corner),
            in_specs=[vmem, vmem],
            out_specs=(vmem, vmem),
            name="head",
            compiler_params=pltpu.CompilerParams(vmem_limit_bytes=GRANT),
        )(mine_a, other_a)
        mine_b, inv_a = lax.optimization_barrier((mine_b, inv_a))
        if back:
            mine_b = mine_b + back[1]
        for bit in bits(scen, 4):
            mine_b = mine_b + swap(mine_b, "scen", scen, bit)
        other_b = swap(mine_b, "scen", scen, 1)
        square = jax.ShapeDtypeStruct((link, link), F32)
        strip, wide, low, inv, wz = pl.pallas_call(
            node_kernel,
            out_shape=(
                jax.ShapeDtypeStruct((2 * share + ROWS, size), F32),
                square,
                square,
                jax.ShapeDtypeStruct((link, size), F32),
                jax.ShapeDtypeStruct((ROWS, link), F32),
            ),
            in_specs=[vmem] * 6 + [anywhere] * scen,
            out_specs=(vmem,) * 5,
            scratch_shapes=[
                pltpu.VMEM((link, link), F32),
                pltpu.VMEM((link, link), F32),
                pltpu.VMEM((3 * size + ROWS, size), F32),
                pltpu.SemaphoreType.DMA((scen,)),
            ],
            name="node",
            compiler_params=pltpu.CompilerParams(vmem_limit_bytes=GRANT),
        )(mine_a, other_a, mine_b, other_b, inv_a, under, *[links[p] for p in range(scen)])
        for bit in bits(node):
            strip = strip + swap(strip, "node", node, bit)
        strips = spread({0: strip}, "scen", scen, down)
        aligned = share % size == 0
        leaf, solved, root = pl.pallas_call(
            root_kernel,
            out_shape=(
                jax.ShapeDtypeStruct((2, order), F32),
                jax.ShapeDtypeStruct((2, share if aligned else link), F32),
                jax.ShapeDtypeStruct((2, link), F32),
            ),
            in_specs=[vmem] * (scen + 9),
            out_specs=(vmem,) * 3,
            scratch_shapes=[
                pltpu.VMEM((link, link), F32),
                pltpu.VMEM((link, link), F32),
                pltpu.VMEM((link, size), F32),
                pltpu.VMEM((link, size), F32),
                pltpu.VMEM((link, size), F32),
                pltpu.VMEM((PARTS * ROWS, size), F32),
                pltpu.VMEM((ROWS, link), F32),
            ],
            name="root",
            compiler_params=pltpu.CompilerParams(vmem_limit_bytes=GRANT),
        )(*[strips[p] for p in range(scen)], root_diag, root_rhs, projected, wide, low, inv, wz, rt, factor)
        if not aligned:
            solved = lax.dynamic_slice(solved, (0, me * share), (2, share))
        return (leaf[None, None], solved[None], root)

    return run


def solution(mesh):
    placed = (
        P("node", "scen", None, None),
        P("node", "scen", None, None),
        P("node", "scen", None, None),
        P("node", "scen", None),
        P("node", None, "scen"),
        P("node", "scen", None),
        P(),
        P(),
    )
    return jax.shard_map(
        build(mesh.shape["scen"], mesh.shape["node"]),
        mesh=mesh,
        in_specs=placed,
        out_specs=(P("node", "scen", None, None), P("node", None, "scen"), P()),
        check_vma=False,
    )
```
